32 devices in a mesh: space: 8 (over y, x, core), vz: 4 (over z).
Axes of the slice: x: 2, y: 2, z: 4, core: 2. Of those that a mesh axis runs over, the one named last changes fastest.
Arguments:
- distribution: float32 [48, 16, 8, 2304], P('vz', 'space'), may hold values from 0 to 6, as said below
- collision_rate: float32 [16, 8], P('space'), may hold values from 0.5 to 2
Outputs:
- new_distribution: float32 [48, 16, 8, 2304], P('vz', 'space')
The draws below stay inside these ranges and needn't reach their ends.
Inputs may be any that keep to these rules, and one draw needn't show every extreme that they name: `distribution`: every entry is positive.
All inputs are finite; a program needn't handle non-finite values.
Results may differ from the reference program's by a relative error of at most 0.000056.
Values sent between devices are 32-bit elements; how exact they have to be, the bound alone decides.
A program may use at most 64 MiB of HBM per device.

```python
import math
import jax
import jax.numpy as jnp
from jax import lax

V = 48
NY = 8
SWEEPS = 3
NX = 16


def draw_distribution(key, part):
    key_list = jax.random.split(key, 6)
    grid_values = 4.5 * (2.0 * jnp.arange(V, dtype=jnp.float32) + 1.0 - V) / V
    speed_x = jnp.repeat(grid_values, V)
    speed_y = jnp.tile(grid_values, V)
    speed_z = grid_values[:, None, None, None]
    cell_shape = (1, NX, NY, 1)
    full_shape = (V, NX, NY, V * V)
    mass_density = jnp.exp(jax.random.uniform(key_list[0], cell_shape, jnp.float32, math.log(0.3), math.log(3.0)))
    roughness = jnp.exp(jax.random.uniform(key_list[1], full_shape, jnp.float32, math.log(0.5), math.log(2.0)))
    spread_t = jnp.exp(jax.random.uniform(key_list[2], cell_shape, jnp.float32, math.log(1.5), math.log(4.0)))
    drift_velocity_x = jax.random.uniform(key_list[3], cell_shape, jnp.float32, -0.8, 0.8)
    drift_velocity_y = jax.random.uniform(key_list[4], cell_shape, jnp.float32, -0.8, 0.8)
    drift_velocity_z = jax.random.uniform(key_list[5], cell_shape, jnp.float32, 0.2, 0.8)
    profile = jnp.exp(-((speed_x - drift_velocity_x) ** 2 + (speed_y - drift_velocity_y) ** 2 + (speed_z - drift_velocity_z) ** 2) / (2.0 * spread_t))
    return (mass_density * profile * roughness).astype(jnp.float32)


def levels(stream_key, shape, shards, smallest, top_value):
    gain, own = 1.0, jax.random.fold_in(stream_key, 6)
    for dim, parts in shards:
        heights = jnp.exp(jax.random.uniform(jax.random.fold_in(own, dim), (parts,), jnp.float32, smallest / len(shards), top_value / len(shards)))
        gain = gain * jnp.repeat(heights, shape[dim] // parts).reshape([-1 if axis == dim else 1 for axis in range(len(shape))])
    return gain


def setup_inputs(seed: int = 0) -> dict:
    key_of = jax.random.split(jax.random.key(seed), 3)
    return {
        "distribution": draw_distribution(jax.random.fold_in(key_of[2], 71), 0),
        "collision_rate": jnp.clip(jnp.exp(math.log(2.0) - 1.3862944 * jax.random.uniform(key_of[1], (NX, NY), jnp.float32) ** levels(key_of[1], (NX, NY), ((0, 8),), -0.2, 0.2)), 0.5, 2.0),
    }


vel_max = 4.5
step_ratio = 0.1
collision_scale = 0.004
relax_scale = 0.5


def grid_speeds(position):
    return vel_max * (2.0 * position + 1.0 - V) / V


def velocity_columns():
    grid_values = grid_speeds(jnp.arange(V, dtype=jnp.float32))
    return jnp.repeat(grid_values, V), jnp.tile(grid_values, V)


def beam_warming(middle, near_cells, far_cells, magnitude):
    return middle - 0.5 * magnitude * (3.0 * middle - 4.0 * near_cells + far_cells) + 0.5 * magnitude * magnitude * (middle - 2.0 * near_cells + far_cells)


def roll_transport(field_data, speed_cols, axis_id):
    positive = speed_cols > 0
    near_cells = jnp.where(positive, jnp.roll(field_data, 1, axis_id), jnp.roll(field_data, -1, axis_id))
    far_cells = jnp.where(positive, jnp.roll(field_data, 2, axis_id), jnp.roll(field_data, -2, axis_id))
    return beam_warming(field_data, near_cells, far_cells, step_ratio * jnp.abs(speed_cols))


def combine_planes(partial_value, vertical_speeds):
    zero_moment = partial_value[0]
    return jnp.stack([jnp.sum(zero_moment, 0), jnp.sum(partial_value[1], 0), jnp.sum(partial_value[2], 0), jnp.sum(vertical_speeds * zero_moment, 0), jnp.sum(partial_value[3] + vertical_speeds * vertical_speeds * zero_moment, 0)])


def cell_state(moment_totals):
    grid_spacing = 2.0 * vel_max / V
    unnormalised_mass = moment_totals[0]
    drift_velocity_x = moment_totals[1] / unnormalised_mass
    drift_velocity_y = moment_totals[2] / unnormalised_mass
    drift_velocity_z = moment_totals[3] / unnormalised_mass
    thermal_energy = (moment_totals[4] / unnormalised_mass - drift_velocity_x * drift_velocity_x - drift_velocity_y * drift_velocity_y - drift_velocity_z * drift_velocity_z) / 3.0
    return unnormalised_mass * grid_spacing ** 3, drift_velocity_x, drift_velocity_y, drift_velocity_z, thermal_energy


def maxwellian(cell_entries, velocity_x_grid, velocity_y_grid, vertical_speeds):
    mass_density, drift_velocity_x, drift_velocity_y, drift_velocity_z, thermal_energy = cell_entries
    squared_spread = (velocity_x_grid - drift_velocity_x) ** 2 + (velocity_y_grid - drift_velocity_y) ** 2 + (vertical_speeds - drift_velocity_z) ** 2
    return mass_density * (2.0 * jnp.pi * thermal_energy) ** -1.5 * jnp.exp(-squared_spread / (2.0 * thermal_energy))


def velocity_shifts(middle):
    zero_row = jnp.zeros(middle.shape[:-1] + (V,), middle.dtype)
    zero_one = jnp.zeros(middle.shape[:-1] + (1,), middle.dtype)
    upper_x_neighbour = jnp.concatenate([middle[..., V:], zero_row], axis=-1)
    lower_x_neighbour = jnp.concatenate([zero_row, middle[..., :-V]], axis=-1)
    upper_y_neighbour = jnp.concatenate([middle[..., 1:], zero_one], axis=-1)
    lower_y_neighbour = jnp.concatenate([zero_one, middle[..., :-1]], axis=-1)
    return upper_x_neighbour, lower_x_neighbour, upper_y_neighbour, lower_y_neighbour


def relaxation_pass(bordered_grid, forcing_term, diagonal_factor, vertical_speeds, cell_entries, collide_rate, velocity_x_grid, velocity_y_grid, upper_mask, lower_mask):
    mass_density, drift_velocity_x, drift_velocity_y, drift_velocity_z, thermal_energy = cell_entries
    grid_spacing = 2.0 * vel_max / V
    stiffness_factor = thermal_energy / (grid_spacing * grid_spacing)
    half_timestep = 0.5 / grid_spacing
    middle = bordered_grid[1:-1]
    upper_x_neighbour, lower_x_neighbour, upper_y_neighbour, lower_y_neighbour = velocity_shifts(middle)
    running_total = forcing_term + collide_rate * ((stiffness_factor + (velocity_x_grid + grid_spacing - drift_velocity_x) * half_timestep) * upper_x_neighbour + (stiffness_factor - (velocity_x_grid - grid_spacing - drift_velocity_x) * half_timestep) * lower_x_neighbour)
    running_total = running_total + collide_rate * ((stiffness_factor + (velocity_y_grid + grid_spacing - drift_velocity_y) * half_timestep) * upper_mask * upper_y_neighbour + (stiffness_factor - (velocity_y_grid - grid_spacing - drift_velocity_y) * half_timestep) * lower_mask * lower_y_neighbour)
    running_total = running_total + collide_rate * ((stiffness_factor + (vertical_speeds + grid_spacing - drift_velocity_z) * half_timestep) * bordered_grid[2:] + (stiffness_factor - (vertical_speeds - grid_spacing - drift_velocity_z) * half_timestep) * bordered_grid[:-2])
    return running_total / diagonal_factor


def reference(distribution, collision_rate):
    velocity_x_grid, velocity_y_grid = velocity_columns()
    weights = jnp.stack([jnp.ones_like(velocity_x_grid), velocity_x_grid, velocity_y_grid, velocity_x_grid * velocity_x_grid + velocity_y_grid * velocity_y_grid], axis=1)

    def transport_plane(plane):
        swept_x = roll_transport(plane, velocity_x_grid, 0)
        partial_sums = jnp.einsum("xyk,kw->wxy", plane, weights, precision=lax.Precision.HIGHEST)
        return roll_transport(swept_x, velocity_y_grid, 1), partial_sums

    transported, partial_value = lax.map(transport_plane, distribution)
    speeds_all = grid_speeds(jnp.arange(V, dtype=jnp.float32))
    moment_totals = combine_planes(jnp.moveaxis(partial_value, 1, 0), speeds_all[:, None, None])
    state_all = cell_state(moment_totals)
    index_y = jnp.arange(V * V, dtype=jnp.int32) % V
    upper_mask = (index_y < V - 1).astype(jnp.float32)
    lower_mask = (index_y > 0).astype(jnp.float32)
    vertical_speeds = speeds_all[:, None, None]
    grid_spacing = 2.0 * vel_max / V

    def column(column_id):
        field_data = lax.dynamic_index_in_dim(transported, column_id, 1, keepdims=False)
        cell_entries = tuple(lax.dynamic_index_in_dim(entry_array, column_id, 0, keepdims=False)[None, :, None] for entry_array in state_all)
        pointwise_rate = lax.dynamic_index_in_dim(collision_rate, column_id, 0, keepdims=False)[None, :, None]
        collide_rate = collision_scale * pointwise_rate
        relaxation_rate = relax_scale * pointwise_rate
        stiffness_factor = cell_entries[4] / (grid_spacing * grid_spacing)
        diagonal_factor = 1.0 + relaxation_rate + 6.0 * collide_rate * stiffness_factor
        forcing_term = field_data + relaxation_rate * maxwellian(cell_entries, velocity_x_grid, velocity_y_grid, vertical_speeds)
        current_guess = field_data
        for sweep_id in range(SWEEPS):
            bordered_grid = jnp.pad(current_guess, ((1, 1), (0, 0), (0, 0)))
            current_guess = relaxation_pass(bordered_grid, forcing_term, diagonal_factor, vertical_speeds, cell_entries, collide_rate, velocity_x_grid, velocity_y_grid, upper_mask, lower_mask)
        return current_guess

    columns = lax.map(column, jnp.arange(NX, dtype=jnp.int32))
    return jnp.moveaxis(columns, 0, 1)
```

```python
import functools

import jax
import jax.numpy as jnp
from jax import lax
from jax.experimental import pallas as pl
from jax.experimental.pallas import tpu as pltpu
from jax.sharding import PartitionSpec as P

V = 48
SWEEPS = 3
HALO = 2
LANES = 128
MESH = pl.DeviceIdType.MESH

vel_max = 4.5
step_ratio = 0.1
collision_scale = 0.004
relax_scale = 0.5
spacing = 2.0 * vel_max / V


def grid_speeds(position):
    return vel_max * (2.0 * position + 1.0 - V) / V


def lane_speeds(first_lane, shape):
    lane = lax.broadcasted_iota(jnp.int32, shape, len(shape) - 1).astype(jnp.float32) + first_lane
    index_x = jnp.floor((lane + 0.5) * (1.0 / V))
    index_y = lane - V * index_x
    return index_x, index_y


def warming_coefficients(speed):
    a = step_ratio * jnp.abs(speed)
    return 1.0 - 1.5 * a + 0.5 * a * a, 2.0 * a - a * a, 0.5 * a * a - 0.5 * a


RDIAG, GAIN, RATE, UP_Z, DOWN_Z, MEAN_Z, HALF_T = range(7)
X0, X1, X2, Y0, Y1, Y2, POS = range(7)
UP_X, DOWN_X, UP_Y, DOWN_Y, GAUSS = range(5)


def kernel(
    space_size,
    vz_size,
    f_hbm,
    rate_hbm,
    out_ref,
    f_ref,
    rate_ref,
    low_ref,
    high_ref,
    t_ref,
    src_ref,
    g1_ref,
    g2_ref,
    lane_ref,
    coef_ref,
    par_ref,
    mom_ref,
    local_sem,
    send_sem,
    recv_sem,
    zsend_sem,
    zrecv_sem,
    msend_sem,
    mrecv_sem,
):
    planes, cols, rows, width = f_ref.shape
    half = width // 2
    tiles = width // LANES
    space = lax.axis_index("space")
    vz = lax.axis_index("vz")
    right = lax.rem(space + 1, space_size)
    left = lax.rem(space + space_size - 1, space_size)
    first_plane = vz * planes
    tile_shape = (rows, LANES)

    f_copy = pltpu.make_async_copy(f_hbm, f_ref, local_sem.at[0])
    rate_copy = pltpu.make_async_copy(rate_hbm, rate_ref, local_sem.at[1])
    f_copy.start()
    rate_copy.start()

    barrier = pltpu.get_barrier_semaphore()
    for neighbour in (left, right):
        pl.semaphore_signal(
            barrier, inc=1, device_id={"space": neighbour}, device_id_type=MESH
        )
    for step in range(1, vz_size):
        pl.semaphore_signal(
            barrier,
            inc=1,
            device_id={"vz": lax.rem(vz + step, vz_size)},
            device_id_type=MESH,
        )
    pl.semaphore_wait(barrier, 2 + vz_size - 1)

    def to_right(p):
        return pltpu.make_async_remote_copy(
            src_ref=f_hbm.at[p, pl.ds(cols - HALO, HALO), :, pl.ds(half, half)],
            dst_ref=low_ref.at[p],
            send_sem=send_sem.at[0, p],
            recv_sem=recv_sem.at[0, p],
            device_id={"space": right},
            device_id_type=MESH,
        )

    def to_left(p):
        return pltpu.make_async_remote_copy(
            src_ref=f_hbm.at[p, pl.ds(0, HALO), :, pl.ds(0, half)],
            dst_ref=high_ref.at[p],
            send_sem=send_sem.at[1, p],
            recv_sem=recv_sem.at[1, p],
            device_id={"space": left},
            device_id_type=MESH,
        )

    def z_down(j):
        return pltpu.make_async_remote_copy(
            src_ref=t_ref.at[SWEEPS + j],
            dst_ref=t_ref.at[planes + SWEEPS + j],
            send_sem=zsend_sem.at[0, j],
            recv_sem=zrecv_sem.at[0, j],
            device_id={"vz": jnp.maximum(vz - 1, 0)},
            device_id_type=MESH,
        )

    def z_up(j):
        return pltpu.make_async_remote_copy(
            src_ref=t_ref.at[planes + SWEEPS - 1 - j],
            dst_ref=t_ref.at[SWEEPS - 1 - j],
            send_sem=zsend_sem.at[1, j],
            recv_sem=zrecv_sem.at[1, j],
            device_id={"vz": jnp.minimum(vz + 1, vz_size - 1)},
            device_id_type=MESH,
        )

    @pl.loop(0, planes // 2)
    def _(i):
        for p in (i, planes - 1 - i):
            to_right(p).start()
            to_left(p).start()

    index_x, index_y = lane_speeds(0.0, (rows, width))
    speed_x, speed_y = grid_speeds(index_x), grid_speeds(index_y)
    for row, value in zip((X0, X1, X2), warming_coefficients(speed_x)):
        lane_ref[row] = value
    for row, value in zip((Y0, Y1, Y2), warming_coefficients(speed_y)):
        lane_ref[row] = value
    lane_ref[POS] = speed_y

    @pl.when(vz == 0)
    def _():
        for ref in (t_ref, g1_ref, g2_ref):
            ref[SWEEPS - 1] = jnp.zeros(ref.shape[1:], jnp.float32)

    @pl.when(vz == vz_size - 1)
    def _():
        for ref in (t_ref, g1_ref, g2_ref):
            ref[planes + SWEEPS] = jnp.zeros(ref.shape[1:], jnp.float32)

    f_copy.wait()
    plane_speeds = [grid_speeds((first_plane + p).astype(jnp.float32)) for p in range(planes)]

    def moment_tile(j, sums):
        tile_x, tile_y = lane_speeds((j * LANES).astype(jnp.float32), tile_shape)
        tile_x, tile_y = grid_speeds(tile_x), grid_speeds(tile_y)
        square = tile_x * tile_x + tile_y * tile_y
        lanes = pl.ds(pl.multiple_of(j * LANES, LANES), LANES)
        result = []
        for c in range(cols):
            total, first, second = 0.0, 0.0, 0.0
            for p in range(planes):
                value = f_ref[p, c, :, lanes]
                moved = value * plane_speeds[p]
                total = total + value
                first = first + moved
                second = second + moved * plane_speeds[p]
            m = sums[5 * c : 5 * c + 5]
            result += [
                m[0] + total,
                m[1] + total * tile_x,
                m[2] + total * tile_y,
                m[3] + first,
                m[4] + total * square + second,
            ]
        return tuple(result)

    zero = jnp.zeros(tile_shape, jnp.float32)
    sums = lax.fori_loop(0, tiles, moment_tile, (zero,) * (5 * cols))
    lane = lax.broadcasted_iota(jnp.int32, tile_shape, 1)
    packed = zero
    for j, value in enumerate(sums):
        packed = jnp.where(lane == j, jnp.sum(value, axis=1, keepdims=True), packed)
    mom_ref[0] = packed

    def moment_copy(step):
        return pltpu.make_async_remote_copy(
            src_ref=mom_ref.at[0],
            dst_ref=mom_ref.at[step],
            send_sem=msend_sem.at[step],
            recv_sem=mrecv_sem.at[step],
            device_id={"vz": lax.rem(vz + step, vz_size)},
            device_id_type=MESH,
        )

    for step in range(1, vz_size):
        moment_copy(step).start()

    def column(p, c, lanes):
        if c < 0:
            return low_ref[p, c + HALO]
        if c >= cols:
            return high_ref[p, c - cols]
        return f_ref[p, c, :, lanes]

    def transport(p):
        back, fore = slice(0, half), slice(half, width)
        for c in range(cols):
            backward = (
                lane_ref[X0, :, back] * f_ref[p, c, :, back]
                + lane_ref[X1, :, back] * column(p, c + 1, back)
                + lane_ref[X2, :, back] * column(p, c + 2, back)
            )
            forward = (
                lane_ref[X0, :, fore] * f_ref[p, c, :, fore]
                + lane_ref[X1, :, fore] * column(p, c - 1, fore)
                + lane_ref[X2, :, fore] * column(p, c - 2, fore)
            )
            for swept, lanes in ((backward, back), (forward, fore)):
                positive = lane_ref[POS, :, lanes] > 0.0
                ahead = pltpu.roll(swept, rows - 2, 0)
                near = pltpu.roll(jnp.where(positive, swept, ahead), 1, 0)
                far = jnp.where(positive, pltpu.roll(swept, 2, 0), ahead)
                t_ref[p + SWEEPS, c, :, lanes] = (
                    lane_ref[Y0, :, lanes] * swept
                    + lane_ref[Y1, :, lanes] * near
                    + lane_ref[Y2, :, lanes] * far
                )

    def pair(i):
        for p in (i, planes - 1 - i):
            to_right(p).wait_recv()
            to_left(p).wait_recv()
            transport(p)

    @pl.loop(0, SWEEPS)
    def _(i):
        pair(i)

        @pl.when(vz > 0)
        def _():
            z_down(i).start()

        @pl.when(vz < vz_size - 1)
        def _():
            z_up(i).start()

    for step in range(1, vz_size):
        moment_copy(step).wait_recv()
    packed = mom_ref[0]
    for step in range(1, vz_size):
        packed = packed + mom_ref[step]
    rate_copy.wait()
    diagonal_mask = lax.broadcasted_iota(jnp.int32, (rows, rows), 0) == lax.broadcasted_iota(
        jnp.int32, (rows, rows), 1
    )

    def spread(value):
        return jnp.concatenate([value] * tiles, axis=1)

    for c in range(cols):
        m0, m1, m2, m3, m4 = (
            jnp.broadcast_to(
                jnp.sum(jnp.where(lane == 5 * c + j, packed, 0.0), axis=1, keepdims=True),
                tile_shape,
            )
            for j in range(5)
        )
        point_rate = jnp.broadcast_to(
            jnp.sum(
                jnp.where(
                    diagonal_mask,
                    jnp.broadcast_to(rate_ref[c : c + 1, :], (rows, rows)),
                    0.0,
                ),
                axis=1,
                keepdims=True,
            ),
            tile_shape,
        )
        ux, uy, uz = m1 / m0, m2 / m0, m3 / m0
        temperature = (m4 / m0 - ux * ux - uy * uy - uz * uz) / 3.0
        density = m0 * spacing**3
        rate = collision_scale * point_rate
        relax = relax_scale * point_rate
        stiff = temperature / (spacing * spacing)
        diagonal = 1.0 + relax + 6.0 * rate * stiff
        scaled = rate / diagonal
        slope = scaled * (0.5 / spacing)
        base = scaled * (stiff + 0.5)
        width_t = 2.0 * jnp.pi * temperature
        half_t = 0.5 / temperature
        par_ref[c, RDIAG] = 1.0 / diagonal
        par_ref[c, GAIN] = relax / diagonal * density / (width_t * jnp.sqrt(width_t))
        par_ref[c, RATE] = slope
        par_ref[c, UP_Z] = base - slope * uz
        par_ref[c, DOWN_Z] = base + slope * uz
        par_ref[c, MEAN_Z] = uz
        par_ref[c, HALF_T] = half_t
        ix, iy = lane_speeds(0.0, (rows, width))
        cx, cy = grid_speeds(ix), grid_speeds(iy)
        coef_ref[c, UP_X] = jnp.where(
            ix < V - 1.5, spread(base - slope * ux) + spread(slope) * cx, 0.0
        )
        coef_ref[c, DOWN_X] = jnp.where(
            ix > 0.5, spread(base + slope * ux) - spread(slope) * cx, 0.0
        )
        coef_ref[c, UP_Y] = jnp.where(
            iy < V - 1.5, spread(base - slope * uy) + spread(slope) * cy, 0.0
        )
        coef_ref[c, DOWN_Y] = jnp.where(
            iy > 0.5, spread(base + slope * uy) - spread(slope) * cy, 0.0
        )
        off_x = cx - spread(ux)
        off_y = cy - spread(uy)
        coef_ref[c, GAUSS] = jnp.exp(-(off_x * off_x + off_y * off_y) * spread(half_t))

    def sweep(level, k):
        b = k + SWEEPS
        old = (t_ref, g1_ref, g2_ref)[level]
        cz = grid_speeds((first_plane + k).astype(jnp.float32))
        for c in range(cols):
            slope = par_ref[c, RATE]
            up_z = spread(par_ref[c, UP_Z] + slope * cz)
            down_z = spread(par_ref[c, DOWN_Z] - slope * cz)
            middle = old[b, c]
            if level == 0:
                off_z = cz - par_ref[c, MEAN_Z]
                gain = par_ref[c, GAIN] * jnp.exp(-off_z * off_z * par_ref[c, HALF_T])
                source = spread(par_ref[c, RDIAG]) * middle + spread(gain) * coef_ref[c, GAUSS]
                src_ref[b, c] = source
            else:
                source = src_ref[b, c]
            total = (
                source
                + up_z * old[b + 1, c]
                + down_z * old[b - 1, c]
                + coef_ref[c, UP_X] * pltpu.roll(middle, width - V, 1)
                + coef_ref[c, DOWN_X] * pltpu.roll(middle, V, 1)
                + coef_ref[c, UP_Y] * pltpu.roll(middle, width - 1, 1)
                + coef_ref[c, DOWN_Y] * pltpu.roll(middle, 1, 1)
            )
            if level == SWEEPS - 1:
                out_ref[k, c] = total
            else:
                (g1_ref, g2_ref)[level][b, c] = total

    def sweep_range(level, low, high):
        if low < 0:
            low = jnp.where(vz == 0, 0, low)
        if high > planes:
            high = jnp.where(vz == vz_size - 1, planes, high)

        @pl.loop(low, high)
        def _(k):
            sweep(level, k)

    last = planes // 2 - 1

    @pl.loop(SWEEPS, last)
    def _(i):
        pair(i)

    @pl.when(vz < vz_size - 1)
    def _():
        for j in range(SWEEPS):
            z_down(j).wait_recv()

    @pl.when(vz > 0)
    def _():
        for j in range(SWEEPS):
            z_up(j).wait_recv()

    for level in range(SWEEPS):
        inner = level + 1
        outer = SWEEPS - 1 - level
        sweep_range(level, -outer, last - inner)
        sweep_range(level, planes - last + inner, planes + outer)

    pair(last)
    for level in range(SWEEPS):
        inner = level + 1
        sweep_range(level, last - inner, planes - last + inner)

    @pl.loop(0, planes)
    def _(p):
        to_right(p).wait_send()
        to_left(p).wait_send()

    for step in range(1, vz_size):
        moment_copy(step).wait_send()

    @pl.when(vz > 0)
    def _():
        for j in range(SWEEPS):
            z_down(j).wait_send()

    @pl.when(vz < vz_size - 1)
    def _():
        for j in range(SWEEPS):
            z_up(j).wait_send()


def solution(mesh):
    space_size, vz_size = mesh.shape["space"], mesh.shape["vz"]

    def shards(distribution, collision_rate):
        planes, cols, rows, width = distribution.shape
        f32 = jnp.float32
        deep = (planes + 2 * SWEEPS, cols, rows, width)
        halo = (planes, HALO, rows, width // 2)
        dma = pltpu.SemaphoreType.DMA
        return pl.pallas_call(
            functools.partial(kernel, space_size, vz_size),
            out_shape=jax.ShapeDtypeStruct(distribution.shape, f32),
            in_specs=[pl.BlockSpec(memory_space=pl.ANY)] * 2,
            out_specs=pl.BlockSpec(memory_space=pltpu.VMEM),
            scratch_shapes=[
                pltpu.VMEM(distribution.shape, f32),
                pltpu.VMEM(collision_rate.shape, f32),
                pltpu.VMEM(halo, f32),
                pltpu.VMEM(halo, f32),
                pltpu.VMEM(deep, f32),
                pltpu.VMEM(deep, f32),
                pltpu.VMEM(deep, f32),
                pltpu.VMEM(deep, f32),
                pltpu.VMEM((7, rows, width), f32),
                pltpu.VMEM((cols, 5, rows, width), f32),
                pltpu.VMEM((cols, 7, rows, LANES), f32),
                pltpu.VMEM((vz_size, rows, LANES), f32),
                dma((2,)),
                dma((2, planes)),
                dma((2, planes)),
                dma((2, SWEEPS)),
                dma((2, SWEEPS)),
                dma((vz_size,)),
                dma((vz_size,)),
            ],
            compiler_params=pltpu.CompilerParams(
                collective_id=0, has_side_effects=True, vmem_limit_bytes=40 * 1024 * 1024
            ),
            name="transport_and_relax",
        )(distribution, collision_rate)

    return jax.shard_map(
        shards,
        mesh=mesh,
        in_specs=(P("vz", "space", None, None), P("space", None)),
        out_specs=P("vz", "space", None, None),
        check_vma=False,
    )
```

```python
import functools

import jax
import jax.numpy as jnp
from jax import lax
from jax.experimental import pallas as pl
from jax.experimental.pallas import tpu as pltpu
from jax.sharding import PartitionSpec as P

V = 48
SWEEPS = 3
HALO = 2
LANES = 128
MESH = pl.DeviceIdType.MESH

vel_max = 4.5
step_ratio = 0.1
collision_scale = 0.004
relax_scale = 0.5
spacing = 2.0 * vel_max / V


def grid_speeds(position):
    return vel_max * (2.0 * position + 1.0 - V) / V


def lane_speeds(first_lane, shape):
    lane = lax.broadcasted_iota(jnp.int32, shape, len(shape) - 1).astype(jnp.float32) + first_lane
    index_x = jnp.floor((lane + 0.5) * (1.0 / V))
    index_y = lane - V * index_x
    return index_x, index_y


def warming_coefficients(speed):
    a = step_ratio * jnp.abs(speed)
    return 1.0 - 1.5 * a + 0.5 * a * a, 2.0 * a - a * a, 0.5 * a * a - 0.5 * a


RDIAG, GAIN, RATE, UP_Z, DOWN_Z, MEAN_Z, HALF_T = range(7)
X0, X1, X2, Y0, Y1, Y2, POS = range(7)
UP_X, DOWN_X, UP_Y, DOWN_Y, GAUSS = range(5)


def kernel(
    space_size,
    vz_size,
    f_hbm,
    rate_hbm,
    out_ref,
    f_ref,
    rate_ref,
    low_ref,
    high_ref,
    t_ref,
    src_ref,
    g1_ref,
    g2_ref,
    lane_ref,
    coef_ref,
    par_ref,
    mom_ref,
    local_sem,
    send_sem,
    recv_sem,
    zsend_sem,
    zrecv_sem,
    msend_sem,
    mrecv_sem,
):
    planes, cols, rows, width = f_ref.shape
    half = width // 2
    tiles = width // LANES
    space = lax.axis_index("space")
    vz = lax.axis_index("vz")
    right = lax.rem(space + 1, space_size)
    left = lax.rem(space + space_size - 1, space_size)
    first_plane = vz * planes
    tile_shape = (rows, LANES)

    f_copy = pltpu.make_async_copy(f_hbm, f_ref, local_sem.at[0])
    rate_copy = pltpu.make_async_copy(rate_hbm, rate_ref, local_sem.at[1])
    f_copy.start()
    rate_copy.start()

    barrier = pltpu.get_barrier_semaphore()
    for neighbour in (left, right):
        pl.semaphore_signal(
            barrier, inc=1, device_id={"space": neighbour}, device_id_type=MESH
        )
    for step in range(1, vz_size):
        pl.semaphore_signal(
            barrier,
            inc=1,
            device_id={"vz": lax.rem(vz + step, vz_size)},
            device_id_type=MESH,
        )
    pl.semaphore_wait(barrier, 2 + vz_size - 1)

    def to_right(p):
        return pltpu.make_async_remote_copy(
            src_ref=f_hbm.at[p, pl.ds(cols - HALO, HALO), :, pl.ds(half, half)],
            dst_ref=low_ref.at[p],
            send_sem=send_sem.at[0, p],
            recv_sem=recv_sem.at[0, p],
            device_id={"space": right},
            device_id_type=MESH,
        )

    def to_left(p):
        return pltpu.make_async_remote_copy(
            src_ref=f_hbm.at[p, pl.ds(0, HALO), :, pl.ds(0, half)],
            dst_ref=high_ref.at[p],
            send_sem=send_sem.at[1, p],
            recv_sem=recv_sem.at[1, p],
            device_id={"space": left},
            device_id_type=MESH,
        )

    def z_down(j):
        return pltpu.make_async_remote_copy(
            src_ref=t_ref.at[SWEEPS + j],
            dst_ref=t_ref.at[planes + SWEEPS + j],
            send_sem=zsend_sem.at[0, j],
            recv_sem=zrecv_sem.at[0, j],
            device_id={"vz": jnp.maximum(vz - 1, 0)},
            device_id_type=MESH,
        )

    def z_up(j):
        return pltpu.make_async_remote_copy(
            src_ref=t_ref.at[planes + SWEEPS - 1 - j],
            dst_ref=t_ref.at[SWEEPS - 1 - j],
            send_sem=zsend_sem.at[1, j],
            recv_sem=zrecv_sem.at[1, j],
            device_id={"vz": jnp.minimum(vz + 1, vz_size - 1)},
            device_id_type=MESH,
        )

    @pl.loop(0, planes // 2)
    def _(i):
        for p in (i, planes - 1 - i):
            to_right(p).start()
            to_left(p).start()

    index_x, index_y = lane_speeds(0.0, (rows, width))
    speed_x, speed_y = grid_speeds(index_x), grid_speeds(index_y)
    for row, value in zip((X0, X1, X2), warming_coefficients(speed_x)):
        lane_ref[row] = value
    for row, value in zip((Y0, Y1, Y2), warming_coefficients(speed_y)):
        lane_ref[row] = value
    lane_ref[POS] = speed_y

    @pl.when(vz == 0)
    def _():
        for ref in (t_ref, g1_ref, g2_ref):
            ref[SWEEPS - 1] = jnp.zeros(ref.shape[1:], jnp.float32)

    @pl.when(vz == vz_size - 1)
    def _():
        for ref in (t_ref, g1_ref, g2_ref):
            ref[planes + SWEEPS] = jnp.zeros(ref.shape[1:], jnp.float32)

    f_copy.wait()
    plane_speeds = [grid_speeds((first_plane + p).astype(jnp.float32)) for p in range(planes)]

    def moment_tile(j, sums):
        tile_x, tile_y = lane_speeds((j * LANES).astype(jnp.float32), tile_shape)
        tile_x, tile_y = grid_speeds(tile_x), grid_speeds(tile_y)
        square = tile_x * tile_x + tile_y * tile_y
        lanes = pl.ds(pl.multiple_of(j * LANES, LANES), LANES)
        result = []
        for c in range(cols):
            total, first, second = 0.0, 0.0, 0.0
            for p in range(planes):
                value = f_ref[p, c, :, lanes]
                moved = value * plane_speeds[p]
                total = total + value
                first = first + moved
                second = second + moved * plane_speeds[p]
            m = sums[5 * c : 5 * c + 5]
            result += [
                m[0] + total,
                m[1] + total * tile_x,
                m[2] + total * tile_y,
                m[3] + first,
                m[4] + total * square + second,
            ]
        return tuple(result)

    zero = jnp.zeros(tile_shape, jnp.float32)
    sums = lax.fori_loop(0, tiles, moment_tile, (zero,) * (5 * cols))
    lane = lax.broadcasted_iota(jnp.int32, tile_shape, 1)
    packed = zero
    for j, value in enumerate(sums):
        packed = jnp.where(lane == j, jnp.sum(value, axis=1, keepdims=True), packed)
    mom_ref[0] = packed

    def moment_copy(step):
        return pltpu.make_async_remote_copy(
            src_ref=mom_ref.at[0],
            dst_ref=mom_ref.at[step],
            send_sem=msend_sem.at[step],
            recv_sem=mrecv_sem.at[step],
            device_id={"vz": lax.rem(vz + step, vz_size)},
            device_id_type=MESH,
        )

    for step in range(1, vz_size):
        moment_copy(step).start()

    def column(p, c, lanes):
        if c < 0:
            return low_ref[p, c + HALO]
        if c >= cols:
            return high_ref[p, c - cols]
        return f_ref[p, c, :, lanes]

    def transport(p):
        back, fore = slice(0, half), slice(half, width)
        for c in range(cols):
            backward = (
                lane_ref[X0, :, back] * f_ref[p, c, :, back]
                + lane_ref[X1, :, back] * column(p, c + 1, back)
                + lane_ref[X2, :, back] * column(p, c + 2, back)
            )
            forward = (
                lane_ref[X0, :, fore] * f_ref[p, c, :, fore]
                + lane_ref[X1, :, fore] * column(p, c - 1, fore)
                + lane_ref[X2, :, fore] * column(p, c - 2, fore)
            )
            for swept, lanes in ((backward, back), (forward, fore)):
                positive = lane_ref[POS, :, lanes] > 0.0
                ahead = pltpu.roll(swept, rows - 2, 0)
                near = pltpu.roll(jnp.where(positive, swept, ahead), 1, 0)
                far = jnp.where(positive, pltpu.roll(swept, 2, 0), ahead)
                t_ref[p + SWEEPS, c, :, lanes] = (
                    lane_ref[Y0, :, lanes] * swept
                    + lane_ref[Y1, :, lanes] * near
                    + lane_ref[Y2, :, lanes] * far
                )

    def arrive(p):
        to_right(p).wait_recv()
        to_left(p).wait_recv()
        transport(p)

    @pl.loop(0, SWEEPS)
    def _(i):
        arrive(i)

        @pl.when(vz > 0)
        def _():
            z_down(i).start()

        arrive(planes - 1 - i)

        @pl.when(vz < vz_size - 1)
        def _():
            z_up(i).start()

    for step in range(1, vz_size):
        moment_copy(step).wait_recv()
    packed = mom_ref[0]
    for step in range(1, vz_size):
        packed = packed + mom_ref[step]
    rate_copy.wait()
    diagonal_mask = lax.broadcasted_iota(jnp.int32, (rows, rows), 0) == lax.broadcasted_iota(
        jnp.int32, (rows, rows), 1
    )

    def spread(value):
        return jnp.concatenate([value] * tiles, axis=1)

    for c in range(cols):
        m0, m1, m2, m3, m4 = (
            jnp.broadcast_to(
                jnp.sum(jnp.where(lane == 5 * c + j, packed, 0.0), axis=1, keepdims=True),
                tile_shape,
            )
            for j in range(5)
        )
        point_rate = jnp.broadcast_to(
            jnp.sum(
                jnp.where(
                    diagonal_mask,
                    jnp.broadcast_to(rate_ref[c : c + 1, :], (rows, rows)),
                    0.0,
                ),
                axis=1,
                keepdims=True,
            ),
            tile_shape,
        )
        ux, uy, uz = m1 / m0, m2 / m0, m3 / m0
        temperature = (m4 / m0 - ux * ux - uy * uy - uz * uz) / 3.0
        density = m0 * spacing**3
        rate = collision_scale * point_rate
        relax = relax_scale * point_rate
        stiff = temperature / (spacing * spacing)
        diagonal = 1.0 + relax + 6.0 * rate * stiff
        scaled = rate / diagonal
        slope = scaled * (0.5 / spacing)
        base = scaled * (stiff + 0.5)
        width_t = 2.0 * jnp.pi * temperature
        half_t = 0.5 / temperature
        par_ref[c, RDIAG] = 1.0 / diagonal
        par_ref[c, GAIN] = relax / diagonal * density / (width_t * jnp.sqrt(width_t))
        par_ref[c, RATE] = slope
        par_ref[c, UP_Z] = base - slope * uz
        par_ref[c, DOWN_Z] = base + slope * uz
        par_ref[c, MEAN_Z] = uz
        par_ref[c, HALF_T] = half_t
        ix, iy = lane_speeds(0.0, (rows, width))
        cx, cy = grid_speeds(ix), grid_speeds(iy)
        coef_ref[c, UP_X] = jnp.where(
            ix < V - 1.5, spread(base - slope * ux) + spread(slope) * cx, 0.0
        )
        coef_ref[c, DOWN_X] = jnp.where(
            ix > 0.5, spread(base + slope * ux) - spread(slope) * cx, 0.0
        )
        coef_ref[c, UP_Y] = jnp.where(
            iy < V - 1.5, spread(base - slope * uy) + spread(slope) * cy, 0.0
        )
        coef_ref[c, DOWN_Y] = jnp.where(
            iy > 0.5, spread(base + slope * uy) - spread(slope) * cy, 0.0
        )
        off_x = cx - spread(ux)
        off_y = cy - spread(uy)
        coef_ref[c, GAUSS] = jnp.exp(-(off_x * off_x + off_y * off_y) * spread(half_t))

    def sweep(level, k):
        b = k + SWEEPS
        old = (t_ref, g1_ref, g2_ref)[level]
        cz = grid_speeds((first_plane + k).astype(jnp.float32))
        for c in range(cols):
            slope = par_ref[c, RATE]
            up_z = spread(par_ref[c, UP_Z] + slope * cz)
            down_z = spread(par_ref[c, DOWN_Z] - slope * cz)
            middle = old[b, c]
            if level == 0:
                off_z = cz - par_ref[c, MEAN_Z]
                gain = par_ref[c, GAIN] * jnp.exp(-off_z * off_z * par_ref[c, HALF_T])
                source = spread(par_ref[c, RDIAG]) * middle + spread(gain) * coef_ref[c, GAUSS]
                src_ref[b, c] = source
            else:
                source = src_ref[b, c]
            total = (
                source
                + up_z * old[b + 1, c]
                + down_z * old[b - 1, c]
                + coef_ref[c, UP_X] * pltpu.roll(middle, width - V, 1)
                + coef_ref[c, DOWN_X] * pltpu.roll(middle, V, 1)
                + coef_ref[c, UP_Y] * pltpu.roll(middle, width - 1, 1)
                + coef_ref[c, DOWN_Y] * pltpu.roll(middle, 1, 1)
            )
            if level == SWEEPS - 1:
                out_ref[k, c] = total
            else:
                (g1_ref, g2_ref)[level][b, c] = total

    def sweep_both(level, items):
        step = items[1] - items[0] if len(items) > 1 else 0

        @pl.loop(0, 2 * len(items))
        def _(n):
            near = items[0] + step * (n // 2)
            far_side = n % 2
            k = near + far_side * (planes - 1 - 2 * near)
            plane = first_plane + k

            @pl.when((plane >= 0) & (plane < planes * vz_size))
            def _():
                sweep(level, k)

    def wait_halo(j):
        @pl.when(vz < vz_size - 1)
        def _():
            z_down(j).wait_recv()

        @pl.when(vz > 0)
        def _():
            z_up(j).wait_recv()

    last = planes // 2 - 1
    done = [(0, 0)] * SWEEPS
    for i in range(SWEEPS - 1, last):
        if i >= SWEEPS:
            arrive(i)
            arrive(planes - 1 - i)
        halos = min(i - SWEEPS + 2, SWEEPS)
        if i - SWEEPS + 1 < SWEEPS:
            wait_halo(i - SWEEPS + 1)
        for level in range(SWEEPS):
            low, high = level + 1 - halos, i - level
            if low < high:
                old_low, old_high = done[level] if done[level][1] > done[level][0] else (low, low)
                items = [*range(low, old_low), *range(old_high, high)]
                for first in range(0, len(items), 2):
                    sweep_both(level, items[first : first + 2])
                done[level] = (low, high)

    arrive(last)
    for level in range(SWEEPS):
        sweep(level, last - 1 - level)
    arrive(planes - 1 - last)
    for level in range(SWEEPS):

        @pl.loop(last - level, planes - last + level + 1)
        def _(k):
            sweep(level, k)

    @pl.loop(0, planes)
    def _(p):
        to_right(p).wait_send()
        to_left(p).wait_send()

    for step in range(1, vz_size):
        moment_copy(step).wait_send()

    @pl.when(vz > 0)
    def _():
        for j in range(SWEEPS):
            z_down(j).wait_send()

    @pl.when(vz < vz_size - 1)
    def _():
        for j in range(SWEEPS):
            z_up(j).wait_send()


def solution(mesh):
    space_size, vz_size = mesh.shape["space"], mesh.shape["vz"]

    def shards(distribution, collision_rate):
        planes, cols, rows, width = distribution.shape
        f32 = jnp.float32
        deep = (planes + 2 * SWEEPS, cols, rows, width)
        halo = (planes, HALO, rows, width // 2)
        dma = pltpu.SemaphoreType.DMA
        return pl.pallas_call(
            functools.partial(kernel, space_size, vz_size),
            out_shape=jax.ShapeDtypeStruct(distribution.shape, f32),
            in_specs=[pl.BlockSpec(memory_space=pl.ANY)] * 2,
            out_specs=pl.BlockSpec(memory_space=pltpu.VMEM),
            scratch_shapes=[
                pltpu.VMEM(distribution.shape, f32),
                pltpu.VMEM(collision_rate.shape, f32),
                pltpu.VMEM(halo, f32),
                pltpu.VMEM(halo, f32),
                pltpu.VMEM(deep, f32),
                pltpu.VMEM(deep, f32),
                pltpu.VMEM(deep, f32),
                pltpu.VMEM(deep, f32),
                pltpu.VMEM((7, rows, width), f32),
                pltpu.VMEM((cols, 5, rows, width), f32),
                pltpu.VMEM((cols, 7, rows, LANES), f32),
                pltpu.VMEM((vz_size, rows, LANES), f32),
                dma((2,)),
                dma((2, planes)),
                dma((2, planes)),
                dma((2, SWEEPS)),
                dma((2, SWEEPS)),
                dma((vz_size,)),
                dma((vz_size,)),
            ],
            compiler_params=pltpu.CompilerParams(
                collective_id=0, has_side_effects=True, vmem_limit_bytes=40 * 1024 * 1024
            ),
            name="transport_and_relax",
        )(*(pltpu.with_memory_space_constraint(x, pltpu.HBM) for x in (distribution, collision_rate)))

    return jax.shard_map(
        shards,
        mesh=mesh,
        in_specs=(P("vz", "space", None, None), P("space", None)),
        out_specs=P("vz", "space", None, None),
        check_vma=False,
    )
```

```python
import functools

import jax
import jax.numpy as jnp
from jax import lax
from jax.experimental import pallas as pl
from jax.experimental.pallas import tpu as pltpu
from jax.sharding import PartitionSpec as P

V = 48
SWEEPS = 3
HALO = 2
LANES = 128
MESH = pl.DeviceIdType.MESH

vel_max = 4.5
step_ratio = 0.1
collision_scale = 0.004
relax_scale = 0.5
spacing = 2.0 * vel_max / V


def grid_speeds(position):
    return vel_max * (2.0 * position + 1.0 - V) / V


def lane_speeds(first_lane, shape):
    lane = lax.broadcasted_iota(jnp.int32, shape, len(shape) - 1).astype(jnp.float32) + first_lane
    index_x = jnp.floor((lane + 0.5) * (1.0 / V))
    index_y = lane - V * index_x
    return index_x, index_y


def warming_coefficients(speed):
    a = step_ratio * jnp.abs(speed)
    return 1.0 - 1.5 * a + 0.5 * a * a, 2.0 * a - a * a, 0.5 * a * a - 0.5 * a


RDIAG, GAIN, RATE, UP_Z, DOWN_Z, MEAN_Z, HALF_T = range(7)
X0, X1, X2, Y0, Y1, Y2, POS = range(7)
UP_X, DOWN_X, UP_Y, DOWN_Y, GAUSS = range(5)


def kernel(
    space_size,
    vz_size,
    f_hbm,
    rate_hbm,
    out_ref,
    f_ref,
    rate_ref,
    low_ref,
    high_ref,
    t_ref,
    src_ref,
    g1_ref,
    g2_ref,
    lane_ref,
    coef_ref,
    par_ref,
    mom_ref,
    local_sem,
    send_sem,
    recv_sem,
    zsend_sem,
    zrecv_sem,
    msend_sem,
    mrecv_sem,
):
    planes, cols, rows, width = f_ref.shape
    half = width // 2
    tiles = width // LANES
    space = lax.axis_index("space")
    vz = lax.axis_index("vz")
    right = lax.rem(space + 1, space_size)
    left = lax.rem(space + space_size - 1, space_size)
    first_plane = vz * planes
    tile_shape = (rows, LANES)

    f_copy = pltpu.make_async_copy(f_hbm, f_ref, local_sem.at[0])
    rate_copy = pltpu.make_async_copy(rate_hbm, rate_ref, local_sem.at[1])

    barrier = pltpu.get_barrier_semaphore()
    for neighbour in (left, right):
        pl.semaphore_signal(
            barrier, inc=1, device_id={"space": neighbour}, device_id_type=MESH
        )
    for step in range(1, vz_size):
        pl.semaphore_signal(
            barrier,
            inc=1,
            device_id={"vz": lax.rem(vz + step, vz_size)},
            device_id_type=MESH,
        )
    pl.semaphore_wait(barrier, 2 + vz_size - 1)

    def to_right(p):
        return pltpu.make_async_remote_copy(
            src_ref=f_hbm.at[p, pl.ds(cols - HALO, HALO), :, pl.ds(half, half)],
            dst_ref=low_ref.at[p],
            send_sem=send_sem.at[0, p],
            recv_sem=recv_sem.at[0, p],
            device_id={"space": right},
            device_id_type=MESH,
        )

    def to_left(p):
        return pltpu.make_async_remote_copy(
            src_ref=f_hbm.at[p, pl.ds(0, HALO), :, pl.ds(0, half)],
            dst_ref=high_ref.at[p],
            send_sem=send_sem.at[1, p],
            recv_sem=recv_sem.at[1, p],
            device_id={"space": left},
            device_id_type=MESH,
        )

    def z_down(j):
        return pltpu.make_async_remote_copy(
            src_ref=t_ref.at[SWEEPS + j],
            dst_ref=t_ref.at[planes + SWEEPS + j],
            send_sem=zsend_sem.at[0, j],
            recv_sem=zrecv_sem.at[0, j],
            device_id={"vz": jnp.maximum(vz - 1, 0)},
            device_id_type=MESH,
        )

    def z_up(j):
        return pltpu.make_async_remote_copy(
            src_ref=t_ref.at[planes + SWEEPS - 1 - j],
            dst_ref=t_ref.at[SWEEPS - 1 - j],
            send_sem=zsend_sem.at[1, j],
            recv_sem=zrecv_sem.at[1, j],
            device_id={"vz": jnp.minimum(vz + 1, vz_size - 1)},
            device_id_type=MESH,
        )

    @pl.loop(0, planes // 2)
    def _(i):
        for p in (i, planes - 1 - i):
            to_right(p).start()
            to_left(p).start()

    f_copy.start()
    rate_copy.start()

    index_x, index_y = lane_speeds(0.0, (rows, width))
    speed_x, speed_y = grid_speeds(index_x), grid_speeds(index_y)
    for row, value in zip((X0, X1, X2), warming_coefficients(speed_x)):
        lane_ref[row] = value
    for row, value in zip((Y0, Y1, Y2), warming_coefficients(speed_y)):
        lane_ref[row] = value
    lane_ref[POS] = speed_y

    @pl.when(vz == 0)
    def _():
        for ref in (t_ref, g1_ref, g2_ref):
            ref[SWEEPS - 1] = jnp.zeros(ref.shape[1:], jnp.float32)

    @pl.when(vz == vz_size - 1)
    def _():
        for ref in (t_ref, g1_ref, g2_ref):
            ref[planes + SWEEPS] = jnp.zeros(ref.shape[1:], jnp.float32)

    f_copy.wait()
    plane_speeds = [grid_speeds((first_plane + p).astype(jnp.float32)) for p in range(planes)]

    def moment_tile(j, sums):
        tile_x, tile_y = lane_speeds((j * LANES).astype(jnp.float32), tile_shape)
        tile_x, tile_y = grid_speeds(tile_x), grid_speeds(tile_y)
        square = tile_x * tile_x + tile_y * tile_y
        lanes = pl.ds(pl.multiple_of(j * LANES, LANES), LANES)
        result = []
        for c in range(cols):
            total, first, second = 0.0, 0.0, 0.0
            for p in range(planes):
                value = f_ref[p, c, :, lanes]
                moved = value * plane_speeds[p]
                total = total + value
                first = first + moved
                second = second + moved * plane_speeds[p]
            m = sums[5 * c : 5 * c + 5]
            result += [
                m[0] + total,
                m[1] + total * tile_x,
                m[2] + total * tile_y,
                m[3] + first,
                m[4] + total * square + second,
            ]
        return tuple(result)

    zero = jnp.zeros(tile_shape, jnp.float32)
    sums = lax.fori_loop(0, tiles, moment_tile, (zero,) * (5 * cols))
    lane = lax.broadcasted_iota(jnp.int32, tile_shape, 1)
    packed = zero
    for j, value in enumerate(sums):
        packed = jnp.where(lane == j, jnp.sum(value, axis=1, keepdims=True), packed)
    mom_ref[0] = packed

    def moment_copy(step):
        return pltpu.make_async_remote_copy(
            src_ref=mom_ref.at[0],
            dst_ref=mom_ref.at[step],
            send_sem=msend_sem.at[step],
            recv_sem=mrecv_sem.at[step],
            device_id={"vz": lax.rem(vz + step, vz_size)},
            device_id_type=MESH,
        )

    for step in range(1, vz_size):
        moment_copy(step).start()

    def column(p, c, lanes):
        if c < 0:
            return low_ref[p, c + HALO]
        if c >= cols:
            return high_ref[p, c - cols]
        return f_ref[p, c, :, lanes]

    def transport(p):
        back, fore = slice(0, half), slice(half, width)
        for c in range(cols):
            backward = (
                lane_ref[X0, :, back] * f_ref[p, c, :, back]
                + lane_ref[X1, :, back] * column(p, c + 1, back)
                + lane_ref[X2, :, back] * column(p, c + 2, back)
            )
            forward = (
                lane_ref[X0, :, fore] * f_ref[p, c, :, fore]
                + lane_ref[X1, :, fore] * column(p, c - 1, fore)
                + lane_ref[X2, :, fore] * column(p, c - 2, fore)
            )
            for swept, lanes in ((backward, back), (forward, fore)):
                positive = lane_ref[POS, :, lanes] > 0.0
                ahead = pltpu.roll(swept, rows - 2, 0)
                near = pltpu.roll(jnp.where(positive, swept, ahead), 1, 0)
                far = jnp.where(positive, pltpu.roll(swept, 2, 0), ahead)
                t_ref[p + SWEEPS, c, :, lanes] = (
                    lane_ref[Y0, :, lanes] * swept
                    + lane_ref[Y1, :, lanes] * near
                    + lane_ref[Y2, :, lanes] * far
                )

    def arrive(p):
        to_right(p).wait_recv()
        to_left(p).wait_recv()
        transport(p)

    @pl.loop(0, SWEEPS)
    def _(i):
        arrive(i)

        @pl.when(vz > 0)
        def _():
            z_down(i).start()

        arrive(planes - 1 - i)

        @pl.when(vz < vz_size - 1)
        def _():
            z_up(i).start()

    for step in range(1, vz_size):
        moment_copy(step).wait_recv()
    packed = mom_ref[0]
    for step in range(1, vz_size):
        packed = packed + mom_ref[step]
    rate_copy.wait()
    diagonal_mask = lax.broadcasted_iota(jnp.int32, (rows, rows), 0) == lax.broadcasted_iota(
        jnp.int32, (rows, rows), 1
    )

    def spread(value):
        return jnp.concatenate([value] * tiles, axis=1)

    for c in range(cols):
        m0, m1, m2, m3, m4 = (
            jnp.broadcast_to(
                jnp.sum(jnp.where(lane == 5 * c + j, packed, 0.0), axis=1, keepdims=True),
                tile_shape,
            )
            for j in range(5)
        )
        point_rate = jnp.broadcast_to(
            jnp.sum(
                jnp.where(
                    diagonal_mask,
                    jnp.broadcast_to(rate_ref[c : c + 1, :], (rows, rows)),
                    0.0,
                ),
                axis=1,
                keepdims=True,
            ),
            tile_shape,
        )
        ux, uy, uz = m1 / m0, m2 / m0, m3 / m0
        temperature = (m4 / m0 - ux * ux - uy * uy - uz * uz) / 3.0
        density = m0 * spacing**3
        rate = collision_scale * point_rate
        relax = relax_scale * point_rate
        stiff = temperature / (spacing * spacing)
        diagonal = 1.0 + relax + 6.0 * rate * stiff
        scaled = rate / diagonal
        slope = scaled * (0.5 / spacing)
        base = scaled * (stiff + 0.5)
        width_t = 2.0 * jnp.pi * temperature
        half_t = 0.5 / temperature
        par_ref[c, RDIAG] = 1.0 / diagonal
        par_ref[c, GAIN] = relax / diagonal * density / (width_t * jnp.sqrt(width_t))
        par_ref[c, RATE] = slope
        par_ref[c, UP_Z] = base - slope * uz
        par_ref[c, DOWN_Z] = base + slope * uz
        par_ref[c, MEAN_Z] = uz
        par_ref[c, HALF_T] = half_t
        ix, iy = lane_speeds(0.0, (rows, width))
        cx, cy = grid_speeds(ix), grid_speeds(iy)
        coef_ref[c, UP_X] = jnp.where(
            ix < V - 1.5, spread(base - slope * ux) + spread(slope) * cx, 0.0
        )
        coef_ref[c, DOWN_X] = jnp.where(
            ix > 0.5, spread(base + slope * ux) - spread(slope) * cx, 0.0
        )
        coef_ref[c, UP_Y] = jnp.where(
            iy < V - 1.5, spread(base - slope * uy) + spread(slope) * cy, 0.0
        )
        coef_ref[c, DOWN_Y] = jnp.where(
            iy > 0.5, spread(base + slope * uy) - spread(slope) * cy, 0.0
        )
        off_x = cx - spread(ux)
        off_y = cy - spread(uy)
        coef_ref[c, GAUSS] = jnp.exp(-(off_x * off_x + off_y * off_y) * spread(half_t))

    def sweep(level, k):
        b = k + SWEEPS
        old = (t_ref, g1_ref, g2_ref)[level]
        cz = grid_speeds((first_plane + k).astype(jnp.float32))
        for c in range(cols):
            slope = par_ref[c, RATE]
            up_z = spread(par_ref[c, UP_Z] + slope * cz)
            down_z = spread(par_ref[c, DOWN_Z] - slope * cz)
            middle = old[b, c]
            if level == 0:
                off_z = cz - par_ref[c, MEAN_Z]
                gain = par_ref[c, GAIN] * jnp.exp(-off_z * off_z * par_ref[c, HALF_T])
                source = spread(par_ref[c, RDIAG]) * middle + spread(gain) * coef_ref[c, GAUSS]
                src_ref[b, c] = source
            else:
                source = src_ref[b, c]
            total = (
                source
                + up_z * old[b + 1, c]
                + down_z * old[b - 1, c]
                + coef_ref[c, UP_X] * pltpu.roll(middle, width - V, 1)
                + coef_ref[c, DOWN_X] * pltpu.roll(middle, V, 1)
                + coef_ref[c, UP_Y] * pltpu.roll(middle, width - 1, 1)
                + coef_ref[c, DOWN_Y] * pltpu.roll(middle, 1, 1)
            )
            if level == SWEEPS - 1:
                out_ref[k, c] = total
            else:
                (g1_ref, g2_ref)[level][b, c] = total

    def sweep_both(level, items):
        step = items[1] - items[0] if len(items) > 1 else 0

        @pl.loop(0, 2 * len(items))
        def _(n):
            near = items[0] + step * (n // 2)
            far_side = n % 2
            k = near + far_side * (planes - 1 - 2 * near)
            plane = first_plane + k

            @pl.when((plane >= 0) & (plane < planes * vz_size))
            def _():
                sweep(level, k)

    def wait_halo(j):
        @pl.when(vz < vz_size - 1)
        def _():
            z_down(j).wait_recv()

        @pl.when(vz > 0)
        def _():
            z_up(j).wait_recv()

    last = planes // 2 - 1
    done = [(0, 0)] * SWEEPS
    for i in range(SWEEPS - 1, last):
        if i >= SWEEPS:
            arrive(i)
            arrive(planes - 1 - i)
        halos = min(i - SWEEPS + 2, SWEEPS)
        if i - SWEEPS + 1 < SWEEPS:
            wait_halo(i - SWEEPS + 1)
        for level in range(SWEEPS):
            low, high = level + 1 - halos, i - level
            if low < high:
                old_low, old_high = done[level] if done[level][1] > done[level][0] else (low, low)
                items = [*range(low, old_low), *range(old_high, high)]
                for first in range(0, len(items), 2):
                    sweep_both(level, items[first : first + 2])
                done[level] = (low, high)

    arrive(last)
    for level in range(SWEEPS):
        sweep(level, last - 1 - level)
    arrive(planes - 1 - last)
    for level in range(SWEEPS):

        @pl.loop(last - level, planes - last + level + 1)
        def _(k):
            sweep(level, k)

    @pl.loop(0, planes)
    def _(p):
        to_right(p).wait_send()
        to_left(p).wait_send()

    for step in range(1, vz_size):
        moment_copy(step).wait_send()

    @pl.when(vz > 0)
    def _():
        for j in range(SWEEPS):
            z_down(j).wait_send()

    @pl.when(vz < vz_size - 1)
    def _():
        for j in range(SWEEPS):
            z_up(j).wait_send()


def solution(mesh):
    space_size, vz_size = mesh.shape["space"], mesh.shape["vz"]

    def shards(distribution, collision_rate):
        planes, cols, rows, width = distribution.shape
        f32 = jnp.float32
        deep = (planes + 2 * SWEEPS, cols, rows, width)
        halo = (planes, HALO, rows, width // 2)
        dma = pltpu.SemaphoreType.DMA
        return pl.pallas_call(
            functools.partial(kernel, space_size, vz_size),
            out_shape=jax.ShapeDtypeStruct(distribution.shape, f32),
            in_specs=[pl.BlockSpec(memory_space=pl.ANY)] * 2,
            out_specs=pl.BlockSpec(memory_space=pltpu.VMEM),
            scratch_shapes=[
                pltpu.VMEM(distribution.shape, f32),
                pltpu.VMEM(collision_rate.shape, f32),
                pltpu.VMEM(halo, f32),
                pltpu.VMEM(halo, f32),
                pltpu.VMEM(deep, f32),
                pltpu.VMEM(deep, f32),
                pltpu.VMEM(deep, f32),
                pltpu.VMEM(deep, f32),
                pltpu.VMEM((7, rows, width), f32),
                pltpu.VMEM((cols, 5, rows, width), f32),
                pltpu.VMEM((cols, 7, rows, LANES), f32),
                pltpu.VMEM((vz_size, rows, LANES), f32),
                dma((2,)),
                dma((2, planes)),
                dma((2, planes)),
                dma((2, SWEEPS)),
                dma((2, SWEEPS)),
                dma((vz_size,)),
                dma((vz_size,)),
            ],
            compiler_params=pltpu.CompilerParams(
                collective_id=0,
                has_side_effects=True,
                vmem_limit_bytes=40 * 1024 * 1024
            ),
            name="transport_and_relax",
        )(*(pltpu.with_memory_space_constraint(x, pltpu.HBM) for x in (distribution, collision_rate)))

    return jax.shard_map(
        shards,
        mesh=mesh,
        in_specs=(P("vz", "space", None, None), P("space", None)),
        out_specs=P("vz", "space", None, None),
        check_vma=False,
    )
```
